1024 devices in a mesh: row: 256 (over y, z, core), col: 4 (over x).
Axes of the slice: x: 4, y: 8, z: 16, core: 2. Of those that a mesh axis runs over, the one named last changes fastest.
Arguments:
- weight: float32 [25600, 5120], P('row', 'col'), may hold values from -6 to 6
- grad: float32 [25600, 5120], P('row', 'col'), may hold values from -6 to 6
- momentum: float32 [25600, 5120], P('row', 'col'), may hold values from -90 to 90
- right_factor: bfloat16 [5120, 256], P('col'), may hold values from -0.078125 to 0.078125
Outputs:
- new_weight: float32 [25600, 5120], P('row', 'col')
- new_momentum: float32 [25600, 5120], P('row', 'col')
- new_right: bfloat16 [5120, 256], P(('col', 'row'))
The draws below stay inside these ranges and needn't reach their ends.
All inputs are finite; a program needn't handle non-finite values.
Results may differ from the reference program's by a relative error of at most 0.0023.
Values sent between devices are 32-bit elements; how exact they have to be, the bound alone decides.
A program may use at most 32 MiB of HBM per device.

```python
import jax
import jax.numpy as jnp
from jax import lax

M = 25600
N = 5120
R = 256


def draw_momentum(key, part):
    first = jax.random.fold_in(key, 11)
    second = jax.random.fold_in(key, 12)
    third = jax.random.fold_in(key, 13)
    row_scale = 3.0 ** (jnp.arange(M, dtype=jnp.float32) / M) * jnp.exp(jax.random.uniform(first, (M,), jnp.float32, 0.0, jnp.log(4.0)))
    col_scale = 3.0 ** (jnp.arange(N, dtype=jnp.float32) / N) * jnp.exp(jax.random.uniform(second, (N,), jnp.float32, 0.0, jnp.log(10.0)))
    values = jax.random.normal(third, (M, N), jnp.float32)
    values = jnp.clip(values, -5.0, 5.0)
    return (values * row_scale[:, None] * col_scale[None, :] / 20.0).astype(jnp.float32)


def shard_levels(stream_key, extent, shards, least, largest):
    def one(position, parts):
        draws = jax.random.uniform(jax.random.fold_in(jax.random.fold_in(stream_key, 6), position), (parts,), jnp.float32, least / len(shards), largest / len(shards))
        return jnp.repeat(jnp.exp(draws), extent[position] // parts).reshape((-1,) + (1,) * (len(extent) - position - 1))

    factor_of = one(*shards[0])
    for cut in shards[1:]:
        factor_of = factor_of * one(*cut)
    return factor_of


def scatter_about(key, shape, width, limit, cuts=(), held_as=jnp.bfloat16):
    gain = shard_levels(key, shape, cuts, -0.22, 0.18) if cuts else 1.0
    drawn = jax.random.normal(key, shape, jnp.float32) * width * gain
    return jnp.minimum(jnp.maximum(drawn, -limit), limit).astype(held_as)


def setup_inputs(seed: int = 0) -> dict:
    arg_keys = jax.random.split(jax.random.key(seed), 5)
    return {
        "weight": scatter_about(arg_keys[0], (M, N), 1.0, 6.0, ((0, 256), (1, 4)), jnp.float32),
        "grad": scatter_about(arg_keys[1], (M, N), 1.0, 6.0, ((0, 256), (1, 4)), jnp.float32),
        "momentum": draw_momentum(jax.random.fold_in(arg_keys[4], 71), 0),
        "right_factor": scatter_about(arg_keys[3], (N, R), N ** -0.5, 0.078125, ((0, 4),)),
    }


feedback_share = 0.05
decay_keep = 0.999
step_rate = 0.5
epsilon = 1e-06

def reference(weight, grad, momentum, right_factor):
    highest = lax.Precision.HIGHEST
    buffer = momentum + grad
    proj = jnp.dot(buffer, right_factor.astype(jnp.float32), precision=highest)
    gram = jnp.dot(proj.T, proj, precision=highest)
    factor = jnp.linalg.cholesky(gram)
    ortho = lax.linalg.triangular_solve(factor, proj, left_side=False, lower=True, transpose_a=True)
    right = jnp.dot(buffer.T, ortho, precision=highest)
    inverse = 1.0 / jnp.sqrt(lax.optimization_barrier(jnp.sum(right * right, axis=0)) + epsilon)
    new_right = (right * inverse).astype(jnp.bfloat16)
    feedback = jnp.dot(ortho, right.T, precision=highest)
    update = jnp.dot(ortho * inverse, right.T, precision=highest)
    new_momentum = buffer - feedback_share * feedback
    scale = (M * N / R) ** 0.5
    new_weight = decay_keep * weight - step_rate * scale * update
    return (new_weight, new_momentum, new_right)
```

```python
import functools

import jax
import jax.numpy as jnp
from jax import lax
from jax.experimental import pallas as pl
from jax.experimental.pallas import tpu as pltpu
from jax.sharding import PartitionSpec as P

M = 25600
N = 5120
R = 256

feedback_share = 0.05
decay_keep = 0.999
step_rate = 0.5
epsilon = 1e-06

CORES = 2
ZL = 4
HALF = 128
F32 = jnp.float32
BF16 = jnp.bfloat16
NN = (((1,), (0,)), ((), ()))
NT = (((1,), (1,)), ((), ()))
TN = (((0,), (0,)), ((), ()))


def exact(a, b, dims):
    return lax.dot_general(a, b, dims, precision=lax.Precision.HIGHEST, preferred_element_type=F32)


def single(a, b, dims):
    return lax.dot_general(a, b, dims, preferred_element_type=F32)


def split(a):
    high = a.astype(BF16)
    return high, (a - high.astype(F32)).astype(BF16)


def triple(a, b, dims):
    ah, al = split(a)
    bh, bl = split(b)
    return single(ah, bh, dims) + (single(ah, bl, dims) + single(al, bh, dims))


def thirds(a):
    high = a.astype(BF16).astype(F32)
    rest = a - high
    middle = rest.astype(BF16).astype(F32)
    return high, middle, rest - middle


def invert_factor(work):
    lane = lax.broadcasted_iota(jnp.int32, (8, HALF), 1)
    sub = lax.broadcasted_iota(jnp.int32, (8, HALF), 0)

    def group(g, carry):
        base = pl.multiple_of(g * 8, 8)
        ra = work[pl.ds(base, 8), 0:HALF]
        rb = work[pl.ds(base, 8), HALF:]
        columns = [
            jnp.broadcast_to(
                jnp.sum(jnp.where(lane == base + i, ra, 0.0), axis=1, keepdims=True), (8, HALF)
            )
            for i in range(8)
        ]
        for i in range(8):
            pivot = jnp.broadcast_to(columns[i][i : i + 1, :], (8, HALF))
            s = lax.rsqrt(pivot)
            s = s * (1.5 - 0.5 * pivot * s * s)
            scaled = columns[i] * s
            below = jnp.where(sub > i, scaled, 0.0)
            for j in range(i + 1, 8):
                columns[j] = columns[j] - below * jnp.broadcast_to(scaled[j : j + 1, :], (8, HALF))
            pa = jnp.broadcast_to(ra[i : i + 1, :], (8, HALF)) * s
            pb = jnp.broadcast_to(rb[i : i + 1, :], (8, HALF)) * s
            ra = jnp.where(sub == i, pa, ra - below * pa)
            rb = jnp.where(sub == i, pb, rb - below * pb)
        work[pl.ds(base, 8), 0:HALF] = ra
        work[pl.ds(base, 8), HALF:] = rb
        masked = jnp.where(lane >= base + 8, ra, 0.0)
        lh, lm, ll = thirds(masked)
        full = jnp.concatenate([ra, rb], axis=1)
        rh, rm, rl = thirds(full)
        left = jnp.concatenate([lh, lh, lm, lh, ll, lm], axis=0).astype(BF16)
        right = jnp.concatenate([rh, rm, rh, rl, rh, rm], axis=0).astype(BF16)
        work[...] = work[...] - single(left, right, TN)
        return carry

    lax.fori_loop(0, HALF // 8, group, 0)


def kernel(
    dims, weight, grad, momentum, factor, new_weight, new_momentum, new_right,
    buf, part, both, rx, wt, cw, accw, yw, ysum, zw, hw, full,
    gp, gc, ga, gy, gz, gh, gfin, work, inv, rt, n0, n1, n2, n3, ssem, rsem,
):
    Y, ZH = dims
    rows = weight.shape[0]
    padded = buf.shape[0]
    span = weight.shape[1] // 2
    ry = HALF // Y
    rc = ry // 2
    rg = 64 // Y
    Z = ZH * ZL
    r = lax.axis_index("row")
    c = lax.axis_index("col")
    core = lax.rem(r, CORES)
    z = lax.rem(r // CORES, Z)
    y = r // (CORES * Z)
    zl = lax.rem(z, ZL)
    zh = z // ZL

    def at(y, z, core, c):
        return {"row": (y * Z + z) * CORES + core, "col": c}

    near = at(y, z, core, c + 1 - 2 * lax.rem(c, 2))
    far = at(y, z, core, 3 - c)
    twin = at(y, z, 1 - core, c)
    ys = [lax.rem(y + d, Y) for d in range(1, Y)]
    zls = [lax.rem(zl + d, ZL) for d in range(1, ZL)]
    zhs = [lax.rem(zh + d, ZH) for d in range(1, ZH)]
    ydev = [at(q, z, core, c) for q in ys]
    zldev = [at(y, zh * ZL + q, core, c) for q in zls]
    zhdev = [at(y, q * ZL + zl, core, c) for q in zhs]

    count = [0]

    def send(src, dst, device):
        k = count[0]
        count[0] += 1
        copy = pltpu.make_async_remote_copy(
            src_ref=src, dst_ref=dst, send_sem=ssem.at[k], recv_sem=rsem.at[k],
            device_id=device, device_id_type=pl.DeviceIdType.MESH,
        )
        copy.start()
        sent.append(copy)
        return copy

    sent = []

    def arrive(copies):
        for copy in copies:
            copy.wait_recv()

    barrier = pltpu.get_barrier_semaphore()
    peers = [near, far, twin] + ydev + zldev + zhdev
    for device in peers:
        pl.semaphore_signal(barrier, inc=1, device_id=device, device_id_type=pl.DeviceIdType.MESH)

    buf[0:rows, :] = momentum[...] + grad[...]
    buf[rows:padded, :] = jnp.zeros((padded - rows, 2 * span), F32)
    value = buf[...]
    bh = value.astype(BF16)
    rest = value - bh.astype(F32)
    bm = rest.astype(BF16)
    bl = (rest - bm.astype(F32)).astype(BF16)
    fr = factor[...]
    partial_value = single(bh, fr, NN) + (single(bm, fr, NN) + single(bl, fr, NN))
    part[0] = partial_value[:, 0:HALF]
    part[1] = partial_value[:, HALF:]
    pl.semaphore_wait(barrier, len(peers))

    one = [send(part.at[0], rx.at[0], near), send(part.at[1], rx.at[1], far)]
    arrive(one)
    both[...] = part[...] + rx[0:2]
    two = [send(both.at[0], rx.at[2], far), send(both.at[1], rx.at[3], near)]
    arrive(two)
    part0 = both[0] + rx[2]
    part1 = both[1] + rx[3]
    proj = jnp.concatenate([part0, part1], axis=1)

    gram = exact(proj, proj, TN)
    gp[0] = gram[:, 0:HALF]
    gp[1] = gram[:, HALF:]
    quarter = pl.multiple_of(c * 64, 64)
    gcopy = send(gp.at[1 - core, pl.ds(quarter, 64)], gc, twin)
    ph, pm = split(proj)
    for h in range(2):
        b_h, b_l = split(buf[:, span * h : span * (h + 1)])
        wt[h] = single(ph, b_h, TN) + (single(ph, b_l, TN) + single(pm, b_h, TN))
    other = pl.multiple_of((1 - core) * HALF, HALF)
    mine = pl.multiple_of(core * HALF, HALF)
    wcopy = send(wt.at[:, pl.ds(other, HALF)], cw, twin)

    arrive([gcopy])
    ga[...] = gp[core, pl.ds(quarter, 64), :] + gc[...]
    gcopies = [
        send(ga.at[pl.ds(pl.multiple_of(q * rg, 8), rg)], gy.at[d], ydev[d]) for d, q in enumerate(ys)
    ]
    arrive([wcopy])
    accw[...] = wt[:, pl.ds(mine, HALF), :] + cw[...]
    wcopies = [
        send(accw.at[:, pl.ds(pl.multiple_of(q * ry, ry), ry)], yw.at[d], ydev[d])
        for d, q in enumerate(ys)
    ]
    arrive(gcopies)
    tile = ga[pl.ds(pl.multiple_of(y * rg, 8), rg), :]
    for d in range(Y - 1):
        tile = tile + gy[d]
    gz[zl] = tile
    gcopies = [send(gz.at[zl], gz.at[zl], device) for device in zldev]
    arrive(gcopies)
    gh[zh] = (gz[0] + gz[1]) + (gz[2] + gz[3])
    gcopies = [send(gh.at[zh], gh.at[zh], device) for device in zhdev]
    arrive(gcopies)
    tile = gh[0]
    for q in range(1, ZH):
        tile = tile + gh[q]
    spot = pl.multiple_of(c * 64 + y * rg, 8)
    gfin[core, pl.ds(spot, rg), :] = tile
    gcopies = [
        send(gfin.at[core, pl.ds(spot, rg)], gfin.at[core, pl.ds(spot, rg)], device) for device in ydev
    ]

    arrive(wcopies)
    block = accw[:, pl.ds(pl.multiple_of(y * ry, ry), ry), :]
    for d in range(Y - 1):
        block = block + yw[d]
    ysum[...] = block
    wcopies = [
        send(
            ysum.at[lax.rem(q, 2), pl.ds(pl.multiple_of((q // 2) * rc, rc), rc)], zw.at[d], zldev[d]
        )
        for d, q in enumerate(zls)
    ]
    arrive(gcopies)
    gcopy = send(
        gfin.at[core, pl.ds(quarter, 64)], gfin.at[core, pl.ds(quarter, 64)], twin
    )
    arrive([gcopy])
    gcopy = send(gfin.at[:, pl.ds(quarter, 64)], gfin.at[:, pl.ds(quarter, 64)], near)
    arrive(wcopies)
    piece = ysum[lax.rem(zl, 2), pl.ds(pl.multiple_of((zl // 2) * rc, rc), rc), :]
    for d in range(ZL - 1):
        piece = piece + zw[d]
    hw[zh] = piece
    wcopies = [send(hw.at[zh], hw.at[zh], device) for device in zhdev]
    arrive([gcopy])
    pair = pl.multiple_of((c // 2) * HALF, HALF)
    gcopy = send(gfin.at[:, pl.ds(pair, HALF)], gfin.at[:, pl.ds(pair, HALF)], far)
    arrive(wcopies)
    piece = hw[0]
    for q in range(1, ZH):
        piece = piece + hw[q]
    spot = pl.multiple_of(core * HALF + y * ry + (zl // 2) * rc, rc)
    hz = lax.rem(zl, 2)
    full[hz, pl.ds(spot, rc), :] = piece
    wcopies = [
        send(full.at[hz, pl.ds(spot, rc)], full.at[hz, pl.ds(spot, rc)], device) for device in zldev
    ]
    arrive(wcopies)
    strip = pl.multiple_of(core * HALF + y * ry, ry)
    wcopies = [
        send(full.at[:, pl.ds(strip, ry)], full.at[:, pl.ds(strip, ry)], device) for device in ydev
    ]
    arrive([gcopy])

    eye = jnp.where(
        lax.broadcasted_iota(jnp.int32, (HALF, HALF), 0)
        == lax.broadcasted_iota(jnp.int32, (HALF, HALF), 1),
        1.0,
        0.0,
    ).astype(F32)
    work[:, 0:HALF] = gfin[0, 0:HALF, :]
    work[:, HALF:] = eye
    invert_factor(work)
    arrive(wcopies)
    wcopy = send(full.at[:, pl.ds(mine, HALF)], full.at[:, pl.ds(mine, HALF)], twin)
    top = work[:, HALF:]
    low = exact(gfin[0, HALF:, :], top, NT)
    inv[0:HALF, 0:HALF] = top
    inv[0:HALF, HALF:] = jnp.zeros((HALF, HALF), F32)
    work[:, 0:HALF] = gfin[1, HALF:, :] - exact(low, low, NT)
    work[:, HALF:] = eye
    cross = exact(low, top, NN)
    invert_factor(work)
    last = work[:, HALF:]
    inv[HALF:, 0:HALF] = -exact(last, cross, NN)
    inv[HALF:, HALF:] = last

    whole = inv[...]
    ortho = triple(proj, whole, NT)
    arrive([wcopy])
    ones = jnp.ones((8, span), F32)
    norms = jnp.zeros((8, R), F32)
    for h in range(2):
        value = triple(whole, full[h], NN)
        rt[h] = value
        norms = norms + exact(ones, value * value, NT)
    n0[...] = norms
    copy = send(n0, n1, near)
    copies = [copy]
    for h in range(2):
        lanes = slice(span * h, span * (h + 1))
        feedback = triple(ortho, rt[h], NN)
        new_momentum[:, lanes] = buf[0:rows, lanes] - feedback_share * feedback[0:rows]
    picked = jnp.zeros((8, R), F32)
    for h in range(2):
        want = 5 * r + lax.broadcasted_iota(jnp.int32, (8, span), 0)
        have = span * h + lax.broadcasted_iota(jnp.int32, (8, span), 1)
        chosen = jnp.where(want == have, 1.0, 0.0).astype(F32)
        picked = picked + exact(chosen, rt[h], NT)
    arrive(copies)
    n2[...] = n0[...] + n1[...]
    copies = [send(n2, n3, far)]
    arrive(copies)
    inverse = 1.0 / jnp.sqrt(n2[...] + n3[...] + epsilon)
    new_right[...] = (picked * inverse)[0:5].astype(BF16)
    scaled = ortho * inverse[0:1, :]
    scale = (M * N / R) ** 0.5
    for h in range(2):
        lanes = slice(span * h, span * (h + 1))
        update = triple(scaled, rt[h], NN)
        new_weight[:, lanes] = decay_keep * weight[:, lanes] - step_rate * scale * update[0:rows]
    for copy in sent:
        copy.wait_send()


def copies_of(Y, ZH):
    return 4 + 2 + 2 * (Y - 1) + 2 * 3 + 2 * (ZH - 1) + (Y - 1) + 1 + 2 + 3 + (Y - 1) + 1 + 2


def on_device(dims, weight, grad, momentum, right_factor):
    Y, ZH = dims
    rows, width = weight.shape
    padded = -(-rows // 8) * 8
    span = width // 2
    ry = HALF // Y
    rc = ry // 2
    rg = 64 // Y
    total = copies_of(Y, ZH)
    vm = lambda *shape: pltpu.VMEM(shape, F32)
    scratch = [
        vm(padded, width), vm(2, padded, HALF), vm(2, padded, HALF), vm(4, padded, HALF),
        vm(2, R, span), vm(2, HALF, span), vm(2, HALF, span), vm(Y - 1, 2, ry, span),
        vm(2, ry, span), vm(ZL - 1, rc, span), vm(ZH, rc, span), vm(2, R, span),
        vm(2, R, HALF), vm(64, HALF), vm(64, HALF), vm(Y - 1, rg, HALF),
        vm(ZL, rg, HALF), vm(ZH, rg, HALF), vm(2, R, HALF), vm(HALF, 2 * HALF), vm(R, R),
        vm(2, R, span), vm(8, R), vm(8, R), vm(8, R), vm(8, R),
        pltpu.SemaphoreType.DMA((total,)), pltpu.SemaphoreType.DMA((total,)),
    ]
    vmem = pl.BlockSpec(memory_space=pltpu.VMEM)
    return pl.pallas_call(
        functools.partial(kernel, dims),
        out_shape=(
            jax.ShapeDtypeStruct((rows, width), F32),
            jax.ShapeDtypeStruct((rows, width), F32),
            jax.ShapeDtypeStruct((5, R), BF16),
        ),
        in_specs=[vmem] * 4,
        out_specs=(vmem,) * 3,
        scratch_shapes=scratch,
        compiler_params=pltpu.CompilerParams(
            collective_id=0, has_side_effects=True, vmem_limit_bytes=60 * 1024 * 1024
        ),
        name="dion_step",
    )(weight, grad, momentum, right_factor)


def solution(mesh):
    placed = (P("row", "col"), P("row", "col"), P("row", "col"), P("col", None))
    return jax.shard_map(
        functools.partial(on_device, (8, 4)),
        mesh=mesh,
        in_specs=placed,
        out_specs=(P("row", "col"), P("row", "col"), P(("col", "row"), None)),
        check_vma=False,
    )
```

```python
import functools

import jax
import jax.numpy as jnp
from jax import lax
from jax.experimental import pallas as pl
from jax.experimental.pallas import tpu as pltpu
from jax.sharding import PartitionSpec as P

M = 25600
N = 5120
R = 256

feedback_share = 0.05
decay_keep = 0.999
step_rate = 0.5
epsilon = 1e-06

CORES = 2
ZL = 4
HALF = 128
F32 = jnp.float32
BF16 = jnp.bfloat16
NN = (((1,), (0,)), ((), ()))
NT = (((1,), (1,)), ((), ()))
TN = (((0,), (0,)), ((), ()))


def exact(a, b, dims):
    return lax.dot_general(a, b, dims, precision=lax.Precision.HIGHEST, preferred_element_type=F32)


def single(a, b, dims):
    return lax.dot_general(a, b, dims, preferred_element_type=F32)


def split(a):
    high = a.astype(BF16)
    return high, (a - high.astype(F32)).astype(BF16)


def triple(a, b, dims):
    ah, al = split(a)
    bh, bl = split(b)
    return single(ah, bh, dims) + (single(ah, bl, dims) + single(al, bh, dims))


def thirds(a):
    high = a.astype(BF16).astype(F32)
    rest = a - high
    middle = rest.astype(BF16).astype(F32)
    return high, middle, rest - middle


def invert_factor(work, first, last):
    lane = lax.broadcasted_iota(jnp.int32, (8, HALF), 1)
    sub = lax.broadcasted_iota(jnp.int32, (8, HALF), 0)

    def group(g, carry):
        base = pl.multiple_of(g * 8, 8)
        ra = work[pl.ds(base, 8), 0:HALF]
        rb = work[pl.ds(base, 8), HALF:]
        columns = [
            jnp.broadcast_to(
                jnp.sum(jnp.where(lane == base + i, ra, 0.0), axis=1, keepdims=True), (8, HALF)
            )
            for i in range(8)
        ]
        for i in range(8):
            pivot = jnp.broadcast_to(columns[i][i : i + 1, :], (8, HALF))
            s = lax.rsqrt(pivot)
            s = s * (1.5 - 0.5 * pivot * s * s)
            scaled = columns[i] * s
            below = jnp.where(sub > i, scaled, 0.0)
            for j in range(i + 1, 8):
                columns[j] = columns[j] - below * jnp.broadcast_to(scaled[j : j + 1, :], (8, HALF))
            pa = jnp.broadcast_to(ra[i : i + 1, :], (8, HALF)) * s
            pb = jnp.broadcast_to(rb[i : i + 1, :], (8, HALF)) * s
            ra = jnp.where(sub == i, pa, ra - below * pa)
            rb = jnp.where(sub == i, pb, rb - below * pb)
        work[pl.ds(base, 8), 0:HALF] = ra
        work[pl.ds(base, 8), HALF:] = rb
        masked = jnp.where(lane >= base + 8, ra, 0.0)
        lh, lm, ll = thirds(masked)
        full = jnp.concatenate([ra, rb], axis=1)
        rh, rm, rl = thirds(full)
        left = jnp.concatenate([lh, lh, lm, lh, ll, lm], axis=0).astype(BF16)
        right = jnp.concatenate([rh, rm, rh, rl, rh, rm], axis=0).astype(BF16)
        work[...] = work[...] - single(left, right, TN)
        return carry

    lax.fori_loop(first, last, group, 0)


def kernel(
    dims, weight, grad, momentum, factor, new_weight, new_momentum, new_right,
    buf, part, both, rx, pr, wt, cw, accw, ring, ysum, zw, hw, full,
    gp, gc, ga, gy, gz, gh, gfin, work, inv, rt, tiles, nz, ssem, rsem,
):
    Y, ZH = dims
    rows = weight.shape[0]
    padded = buf.shape[0]
    span = weight.shape[1] // 2
    ry = HALF // Y
    rc = ry // 2
    rg = 64 // Y
    Z = ZH * ZL
    r = lax.axis_index("row")
    c = lax.axis_index("col")
    core = lax.rem(r, CORES)
    z = lax.rem(r // CORES, Z)
    y = r // (CORES * Z)
    zl = lax.rem(z, ZL)
    zh = z // ZL

    def at(y, z, core, c):
        return {"row": (y * Z + z) * CORES + core, "col": c}

    near = at(y, z, core, c + 1 - 2 * lax.rem(c, 2))
    far = at(y, z, core, 3 - c)
    twin = at(y, z, 1 - core, c)
    xdev = [at(y, z, core, lax.rem(c + d, 4)) for d in range(1, 4)]
    ys = [lax.rem(y + d, Y) for d in range(1, Y)]
    zls = [lax.rem(zl + d, ZL) for d in range(1, ZL)]
    zhs = [lax.rem(zh + d, ZH) for d in range(1, ZH)]
    ydev = [at(q, z, core, c) for q in ys]
    zldev = [at(y, zh * ZL + q, core, c) for q in zls]
    zhdev = [at(y, q * ZL + zl, core, c) for q in zhs]
    up, down = at(lax.rem(y + 1, Y), z, core, c), at(lax.rem(y + Y - 1, Y), z, core, c)
    hops = {(0, 1): Y // 2, (1, -1): Y // 2, (1, 1): Y // 2 - 1, (0, -1): Y // 2 - 1}
    ways = [w for w in hops if hops[w]]

    count = [0]
    sent = []

    def send(src, dst, device):
        k = count[0]
        count[0] += 1
        copy = pltpu.make_async_remote_copy(
            src_ref=src, dst_ref=dst, send_sem=ssem.at[k], recv_sem=rsem.at[k],
            device_id=device, device_id_type=pl.DeviceIdType.MESH,
        )
        copy.start()
        sent.append(copy)
        return copy

    def arrive(copies):
        for copy in copies:
            copy.wait_recv()

    barrier = pltpu.get_barrier_semaphore()
    peers = xdev + [twin] + ydev + zldev + zhdev
    for device in peers:
        pl.semaphore_signal(barrier, inc=1, device_id=device, device_id_type=pl.DeviceIdType.MESH)

    buf[0:rows, :] = momentum[...] + grad[...]
    buf[rows:padded, :] = jnp.zeros((padded - rows, 2 * span), F32)
    value = buf[...]
    bh = value.astype(BF16)
    rest = value - bh.astype(F32)
    bm = rest.astype(BF16)
    bl = (rest - bm.astype(F32)).astype(BF16)
    fr = factor[...]
    partial_value = single(bh, fr, NN) + (single(bm, fr, NN) + single(bl, fr, NN))
    part[0] = partial_value[:, 0:HALF]
    part[1] = partial_value[:, HALF:]
    pl.semaphore_wait(barrier, len(peers))

    one = [send(part.at[0], rx.at[0], near), send(part.at[1], rx.at[1], far)]
    arrive(one)
    both[...] = part[...] + rx[0:2]
    two = [send(both.at[0], rx.at[2], far), send(both.at[1], rx.at[3], near)]
    arrive(two)
    pr[0] = both[0] + rx[2]
    pr[1] = both[1] + rx[3]
    proj = jnp.concatenate([pr[0], pr[1]], axis=1)

    gram = exact(proj, proj, TN)
    gp[0] = gram[:, 0:HALF]
    gp[1] = gram[:, HALF:]
    quarter = pl.multiple_of(c * 64, 64)
    gcopy = send(gp.at[1 - core, pl.ds(quarter, 64)], gc, twin)
    mine = pl.multiple_of(core * HALF, HALF)
    ph, pm = split(pr[1 - core])
    wcopies = []
    for h in range(2):
        b_h, b_l = split(buf[:, span * h : span * (h + 1)])
        wt[h] = single(ph, b_h, TN) + (single(ph, b_l, TN) + single(pm, b_h, TN))
        wcopies.append(send(wt.at[h], cw.at[h], twin))
    ph, pm = split(pr[core])
    for h in range(2):
        b_h, b_l = split(buf[:, span * h : span * (h + 1)])
        accw[h] = single(ph, b_h, TN) + (single(ph, b_l, TN) + single(pm, b_h, TN))
    arrive([gcopy])
    ga[...] = gp[core, pl.ds(quarter, 64), :] + gc[...]
    gcopies = [
        send(ga.at[pl.ds(pl.multiple_of(q * rg, 8), rg)], gy.at[d], ydev[d]) for d, q in enumerate(ys)
    ]

    def chunk(h, sign, left):
        q = lax.rem(y + sign * left + Y, Y)
        return accw.at[h, pl.ds(pl.multiple_of(q * ry, ry), ry)]

    slots = {}
    for w in ways:
        for step in range(1, hops[w] + 1):
            slots[w + (step,)] = len(slots)
    flying = {}

    def pass_on(w, step):
        h, sign = w
        if step > 1:
            arrive([flying[w]])
            ref = chunk(h, sign, hops[w] + 1 - step)
            ref[...] = ref[...] + ring[slots[w + (step - 1,)]]
        flying[w] = send(
            chunk(h, sign, hops[w] + 1 - step), ring.at[slots[w + (step,)]], up if sign > 0 else down
        )

    for h in range(2):
        arrive([wcopies[h]])
        accw[h] = accw[h] + cw[h]
        for w in ways:
            if w[0] == h:
                pass_on(w, 1)

    def ring_step(step):
        for w in ways:
            if hops[w] >= step:
                pass_on(w, step)

    ring_step(2)
    arrive(gcopies)
    tile = ga[pl.ds(pl.multiple_of(y * rg, 8), rg), :]
    for d in range(Y - 1):
        tile = tile + gy[d]
    gz[zl] = tile
    gcopies = [send(gz.at[zl], gz.at[zl], device) for device in zldev]
    ring_step(3)
    arrive(gcopies)
    gh[zh] = (gz[0] + gz[1]) + (gz[2] + gz[3])
    gcopies = [send(gh.at[zh], gh.at[zh], device) for device in zhdev]
    ring_step(4)
    own = pl.multiple_of(y * ry, ry)
    for h in range(2):
        block = accw[h, pl.ds(own, ry), :]
        for w in ways:
            if w[0] == h:
                arrive([flying[w]])
                block = block + ring[slots[w + (hops[w],)]]
        ysum[h] = block
    wcopies = [
        send(
            ysum.at[lax.rem(q, 2), pl.ds(pl.multiple_of((q // 2) * rc, rc), rc)], zw.at[d], zldev[d]
        )
        for d, q in enumerate(zls)
    ]
    arrive(gcopies)
    tile = gh[0]
    for q in range(1, ZH):
        tile = tile + gh[q]
    spot = pl.multiple_of(c * 64 + y * rg, 8)
    gfin[core, pl.ds(spot, rg), :] = tile
    gcopies = [
        send(gfin.at[core, pl.ds(spot, rg)], gfin.at[core, pl.ds(spot, rg)], device)
        for device in ydev
    ]
    arrive(wcopies)
    piece = ysum[lax.rem(zl, 2), pl.ds(pl.multiple_of((zl // 2) * rc, rc), rc), :]
    for d in range(ZL - 1):
        piece = piece + zw[d]
    hw[zh] = piece
    wcopies = [send(hw.at[zh], hw.at[zh], device) for device in zhdev]
    arrive(gcopies)
    gcopy = send(gfin.at[core, pl.ds(quarter, 64)], gfin.at[core, pl.ds(quarter, 64)], twin)
    arrive([gcopy])
    gcopy = send(gfin.at[:, pl.ds(quarter, 64)], gfin.at[:, pl.ds(quarter, 64)], near)
    arrive([gcopy])
    pair = pl.multiple_of((c // 2) * HALF, HALF)
    gcopy = send(gfin.at[:, pl.ds(pair, HALF)], gfin.at[:, pl.ds(pair, HALF)], far)
    arrive(wcopies)
    piece = hw[0]
    for q in range(1, ZH):
        piece = piece + hw[q]
    spot = pl.multiple_of(core * HALF + y * ry + (zl // 2) * rc, rc)
    hz = lax.rem(zl, 2)
    full[hz, pl.ds(spot, rc), :] = piece
    wcopies = [
        send(full.at[hz, pl.ds(spot, rc)], full.at[hz, pl.ds(spot, rc)], device) for device in zldev
    ]
    arrive([gcopy])

    eye = jnp.where(
        lax.broadcasted_iota(jnp.int32, (HALF, HALF), 0)
        == lax.broadcasted_iota(jnp.int32, (HALF, HALF), 1),
        1.0,
        0.0,
    ).astype(F32)
    work[:, 0:HALF] = gfin[0, 0:HALF, :]
    work[:, HALF:] = eye
    invert_factor(work, 0, 5)
    arrive(wcopies)

    def strip(h, sign, away):
        q = lax.rem(y - sign * away + Y, Y)
        return full.at[h, pl.ds(pl.multiple_of(mine + q * ry, ry), ry)]

    handed = []
    flying = {}

    def share(w, step):
        h, sign = w
        if step > 1:
            arrive([flying[w]])
        ref = strip(h, sign, step - 1)
        if step <= hops[w]:
            flying[w] = send(ref, ref, up if sign > 0 else down)
        if step > 1 or w in ((0, 1), (1, -1)):
            handed.append(send(ref, ref, twin))

    def share_step(step):
        for w in ways:
            if hops[w] + 1 >= step:
                share(w, step)

    share_step(1)
    invert_factor(work, 5, 10)
    share_step(2)
    invert_factor(work, 10, 16)
    share_step(3)
    top = work[:, HALF:]
    low = exact(gfin[0, HALF:, :], top, NT)
    inv[0:HALF, 0:HALF] = top
    inv[0:HALF, HALF:] = jnp.zeros((HALF, HALF), F32)
    work[:, 0:HALF] = gfin[1, HALF:, :] - exact(low, low, NT)
    work[:, HALF:] = eye
    cross = exact(low, top, NN)
    share_step(4)
    invert_factor(work, 0, 5)
    share_step(5)
    invert_factor(work, 5, 16)
    last = work[:, HALF:]
    inv[HALF:, 0:HALF] = -exact(last, cross, NN)
    inv[HALF:, HALF:] = last

    whole = inv[...]
    arrive(handed)
    lanes_sum = jnp.zeros((R, HALF), F32)
    for h in range(2):
        value = triple(whole, full[h], NN)
        rt[h] = value
        for j in range(span // HALF):
            piece = value[:, HALF * j : HALF * (j + 1)]
            tiles[(span // HALF) * h + j] = piece
            lanes_sum = lanes_sum + piece * piece
    nz[c] = exact(jnp.ones((8, HALF), F32), lanes_sum, NT)
    copies = [send(nz.at[c], nz.at[c], device) for device in xdev]
    ortho = triple(proj, whole, NT)
    for h in range(2):
        lanes = slice(span * h, span * (h + 1))
        feedback = triple(ortho, rt[h], NN)
        new_momentum[:, lanes] = buf[0:rows, lanes] - feedback_share * feedback[0:rows]
    want = 5 * r + lax.broadcasted_iota(jnp.int32, (8, HALF), 0)
    have = lax.broadcasted_iota(jnp.int32, (8, HALF), 1)
    spot = (5 * r) // HALF
    picked = jnp.zeros((8, R), F32)
    for k in range(2):
        chosen = jnp.where(want == have + HALF * (spot + k), 1.0, 0.0).astype(F32)
        picked = picked + exact(chosen, tiles[jnp.minimum(spot + k, 2 * span // HALF - 1)], NT)
    arrive(copies)
    inverse = 1.0 / jnp.sqrt(((nz[0] + nz[1]) + (nz[2] + nz[3])) + epsilon)
    new_right[...] = (picked * inverse)[0:5].astype(BF16)
    scaled = ortho * inverse[0:1, :]
    scale = (M * N / R) ** 0.5
    for h in range(2):
        lanes = slice(span * h, span * (h + 1))
        update = triple(scaled, rt[h], NN)
        new_weight[:, lanes] = decay_keep * weight[:, lanes] - step_rate * scale * update[0:rows]
    for copy in sent:
        copy.wait_send()


def copies_of(Y, ZH):
    return 4 + 1 + 2 + 4 * (Y - 1) + 4 * 3 + 2 * (ZH - 1) + 3 + 3 + 2 * (Y - 1) + 2 * Y + 16


def on_device(dims, weight, grad, momentum, right_factor):
    Y, ZH = dims
    rows, width = weight.shape
    padded = -(-rows // 8) * 8
    span = width // 2
    ry = HALF // Y
    rc = ry // 2
    rg = 64 // Y
    total = copies_of(Y, ZH)
    vm = lambda *shape: pltpu.VMEM(shape, F32)
    scratch = [
        vm(padded, width), vm(2, padded, HALF), vm(2, padded, HALF), vm(4, padded, HALF),
        vm(2, padded, HALF), vm(2, HALF, span), vm(2, HALF, span), vm(2, HALF, span),
        vm(2 * (Y - 1), ry, span), vm(2, ry, span), vm(ZL - 1, rc, span), vm(ZH, rc, span),
        vm(2, R, span), vm(2, R, HALF), vm(64, HALF), vm(64, HALF), vm(Y - 1, rg, HALF),
        vm(ZL, rg, HALF), vm(ZH, rg, HALF), vm(2, R, HALF), vm(HALF, 2 * HALF), vm(R, R),
        vm(2, R, span), vm(width // HALF, R, HALF), vm(4, 8, R),
        pltpu.SemaphoreType.DMA((total,)), pltpu.SemaphoreType.DMA((total,)),
    ]
    vmem = pl.BlockSpec(memory_space=pltpu.VMEM)
    return pl.pallas_call(
        functools.partial(kernel, dims),
        out_shape=(
            jax.ShapeDtypeStruct((rows, width), F32),
            jax.ShapeDtypeStruct((rows, width), F32),
            jax.ShapeDtypeStruct((5, R), BF16),
        ),
        in_specs=[vmem] * 4,
        out_specs=(vmem,) * 3,
        scratch_shapes=scratch,
        compiler_params=pltpu.CompilerParams(
            collective_id=0, has_side_effects=True, vmem_limit_bytes=60 * 1024 * 1024
        ),
        name="dion_step",
    )(weight, grad, momentum, right_factor)


def solution(mesh):
    placed = (P("row", "col"), P("row", "col"), P("row", "col"), P("col", None))
    return jax.shard_map(
        functools.partial(on_device, (8, 4)),
        mesh=mesh,
        in_specs=placed,
        out_specs=(P("row", "col"), P("row", "col"), P(("col", "row"), None)),
        check_vma=False,
    )
```

```python
import functools

import jax
import jax.numpy as jnp
from jax import lax
from jax.experimental import pallas as pl
from jax.experimental.pallas import tpu as pltpu
from jax.sharding import PartitionSpec as P

M = 25600
N = 5120
R = 256

feedback_share = 0.05
decay_keep = 0.999
step_rate = 0.5
epsilon = 1e-06

CORES = 2
ZL = 4
HALF = 128
F32 = jnp.float32
BF16 = jnp.bfloat16
NN = (((1,), (0,)), ((), ()))
NT = (((1,), (1,)), ((), ()))
TN = (((0,), (0,)), ((), ()))


def exact(a, b, dims):
    return lax.dot_general(a, b, dims, precision=lax.Precision.HIGHEST, preferred_element_type=F32)


def single(a, b, dims):
    return lax.dot_general(a, b, dims, preferred_element_type=F32)


def split(a):
    high = a.astype(BF16)
    return high, (a - high.astype(F32)).astype(BF16)


def triple(a, b, dims):
    ah, al = split(a)
    bh, bl = split(b)
    return single(ah, bh, dims) + (single(ah, bl, dims) + single(al, bh, dims))


def thirds(a):
    high = a.astype(BF16).astype(F32)
    rest = a - high
    middle = rest.astype(BF16).astype(F32)
    return high, middle, rest - middle


def invert_factor(work, first, last):
    lane = lax.broadcasted_iota(jnp.int32, (8, HALF), 1)
    sub = lax.broadcasted_iota(jnp.int32, (8, HALF), 0)

    def group(g, carry):
        base = pl.multiple_of(g * 8, 8)
        ra = work[pl.ds(base, 8), 0:HALF]
        rb = work[pl.ds(base, 8), HALF:]
        columns = [
            jnp.broadcast_to(
                jnp.sum(jnp.where(lane == base + i, ra, 0.0), axis=1, keepdims=True), (8, HALF)
            )
            for i in range(8)
        ]
        for i in range(8):
            pivot = jnp.broadcast_to(columns[i][i : i + 1, :], (8, HALF))
            s = lax.rsqrt(pivot)
            s = s * (1.5 - 0.5 * pivot * s * s)
            scaled = columns[i] * s
            below = jnp.where(sub > i, scaled, 0.0)
            for j in range(i + 1, 8):
                columns[j] = columns[j] - below * jnp.broadcast_to(scaled[j : j + 1, :], (8, HALF))
            pa = jnp.broadcast_to(ra[i : i + 1, :], (8, HALF)) * s
            pb = jnp.broadcast_to(rb[i : i + 1, :], (8, HALF)) * s
            ra = jnp.where(sub == i, pa, ra - below * pa)
            rb = jnp.where(sub == i, pb, rb - below * pb)
        work[pl.ds(base, 8), 0:HALF] = ra
        work[pl.ds(base, 8), HALF:] = rb
        masked = jnp.where(lane >= base + 8, ra, 0.0)
        lh, lm, ll = thirds(masked)
        full = jnp.concatenate([ra, rb], axis=1)
        rh, rm, rl = thirds(full)
        left = jnp.concatenate([lh, lh, lm, lh, ll, lm], axis=0).astype(BF16)
        right = jnp.concatenate([rh, rm, rh, rl, rh, rm], axis=0).astype(BF16)
        work[...] = work[...] - single(left, right, TN)
        return carry

    lax.fori_loop(first, last, group, 0)


def kernel(
    dims, weight, grad, momentum, factor, new_weight, new_momentum, new_right,
    buf, part, both, rx, pr, wt, cw, accw, ring, ysum, zw, hw, full,
    gp, gy, gz, gh, gfin, work, inv, rt, tiles, nz, ssem, rsem,
):
    Y, ZH = dims
    rows = weight.shape[0]
    padded = buf.shape[0]
    span = weight.shape[1] // 2
    ry = HALF // Y
    rc = ry // 2
    rg = 64 // Y
    Z = ZH * ZL
    r = lax.axis_index("row")
    c = lax.axis_index("col")
    core = lax.rem(r, CORES)
    z = lax.rem(r // CORES, Z)
    y = r // (CORES * Z)
    zl = lax.rem(z, ZL)
    zh = z // ZL

    def at(y, z, core, c):
        return {"row": (y * Z + z) * CORES + core, "col": c}

    near = at(y, z, core, c + 1 - 2 * lax.rem(c, 2))
    far = at(y, z, core, 3 - c)
    twin = at(y, z, 1 - core, c)
    xdev = [at(y, z, core, lax.rem(c + d, 4)) for d in range(1, 4)]
    zls = [lax.rem(zl + d, ZL) for d in range(1, ZL)]
    zhs = [lax.rem(zh + d, ZH) for d in range(1, ZH)]
    group = [(d, k) for d in range(Y) for k in range(CORES) if d or k]
    gdev = []
    for d, k in group:
        gdev.append((lax.rem(y + d, Y), 1 - core if k else core))
    gsend = [at(q, z, k, c) for q, k in gdev]
    zldev = [at(y, zh * ZL + q, core, c) for q in zls]
    zhdev = [at(y, q * ZL + zl, core, c) for q in zhs]
    up, down = at(lax.rem(y + 1, Y), z, core, c), at(lax.rem(y + Y - 1, Y), z, core, c)
    hops = {(0, 1): Y // 2, (1, -1): Y // 2, (1, 1): Y // 2 - 1, (0, -1): Y // 2 - 1}
    ways = [w for w in hops if hops[w]]

    count = [0]
    sent = []

    def send(src, dst, device):
        k = count[0]
        count[0] += 1
        copy = pltpu.make_async_remote_copy(
            src_ref=src, dst_ref=dst, send_sem=ssem.at[k], recv_sem=rsem.at[k],
            device_id=device, device_id_type=pl.DeviceIdType.MESH,
        )
        copy.start()
        sent.append(copy)
        return copy

    def arrive(copies):
        for copy in copies:
            copy.wait_recv()

    barrier = pltpu.get_barrier_semaphore()
    peers = xdev + gsend + zldev + zhdev
    for device in peers:
        pl.semaphore_signal(barrier, inc=1, device_id=device, device_id_type=pl.DeviceIdType.MESH)

    buf[0:rows, :] = momentum[...] + grad[...]
    buf[rows:padded, :] = jnp.zeros((padded - rows, 2 * span), F32)
    value = buf[...]
    bh = value.astype(BF16)
    rest = value - bh.astype(F32)
    bm = rest.astype(BF16)
    bl = (rest - bm.astype(F32)).astype(BF16)
    fr = factor[...]
    partial_value = single(bh, fr, NN) + (single(bm, fr, NN) + single(bl, fr, NN))
    part[0] = partial_value[:, 0:HALF]
    part[1] = partial_value[:, HALF:]
    pl.semaphore_wait(barrier, len(peers))

    one = [send(part.at[0], rx.at[0], near), send(part.at[1], rx.at[1], far)]
    arrive(one)
    both[...] = part[...] + rx[0:2]
    two = [send(both.at[0], rx.at[2], far), send(both.at[1], rx.at[3], near)]
    arrive(two)
    pr[0] = both[0] + rx[2]
    pr[1] = both[1] + rx[3]
    proj = jnp.concatenate([pr[0], pr[1]], axis=1)

    gram = exact(pr[c // 2], proj, TN)
    gp[0] = gram[:, 0:HALF]
    gp[1] = gram[:, HALF:]
    inner = lax.rem(c, 2) * 64
    gcopies = [
        send(gp.at[k, pl.ds(pl.multiple_of(inner + q * rg, 8), rg)], gy.at[d], gsend[d])
        for d, (q, k) in enumerate(gdev)
    ]
    mine = pl.multiple_of(core * HALF, HALF)
    ph, pm = split(pr[1 - core])
    wcopies = []
    for h in range(2):
        b_h, b_l = split(buf[:, span * h : span * (h + 1)])
        wt[h] = single(ph, b_h, TN) + (single(ph, b_l, TN) + single(pm, b_h, TN))
        wcopies.append(send(wt.at[h], cw.at[h], twin))
    ph, pm = split(pr[core])
    for h in range(2):
        b_h, b_l = split(buf[:, span * h : span * (h + 1)])
        accw[h] = single(ph, b_h, TN) + (single(ph, b_l, TN) + single(pm, b_h, TN))
    arrive(gcopies)
    tile = gp[core, pl.ds(pl.multiple_of(inner + y * rg, 8), rg), :]
    for d in range(len(group)):
        tile = tile + gy[d]
    gz[zl] = tile
    gcopies = [send(gz.at[zl], gz.at[zl], device) for device in zldev]

    def chunk(h, sign, left):
        q = lax.rem(y + sign * left + Y, Y)
        return accw.at[h, pl.ds(pl.multiple_of(q * ry, ry), ry)]

    slots = {}
    for w in ways:
        for step in range(1, hops[w] + 1):
            slots[w + (step,)] = len(slots)
    flying = {}

    def pass_on(w, step):
        h, sign = w
        if step > 1:
            arrive([flying[w]])
            ref = chunk(h, sign, hops[w] + 1 - step)
            ref[...] = ref[...] + ring[slots[w + (step - 1,)]]
        flying[w] = send(
            chunk(h, sign, hops[w] + 1 - step), ring.at[slots[w + (step,)]], up if sign > 0 else down
        )

    for h in range(2):
        arrive([wcopies[h]])
        accw[h] = accw[h] + cw[h]
        for w in ways:
            if w[0] == h:
                pass_on(w, 1)

    def ring_step(step):
        for w in ways:
            if hops[w] >= step:
                pass_on(w, step)

    ring_step(2)
    arrive(gcopies)
    gh[zh] = (gz[0] + gz[1]) + (gz[2] + gz[3])
    gcopies = [send(gh.at[zh], gh.at[zh], device) for device in zhdev]
    ring_step(3)
    ring_step(4)
    arrive(gcopies)
    tile = gh[0]
    for q in range(1, ZH):
        tile = tile + gh[q]
    spot = pl.multiple_of(c * 64 + y * rg, 8)
    gfin[core, pl.ds(spot, rg), :] = tile
    gcopies = [
        send(gfin.at[core, pl.ds(spot, rg)], gfin.at[core, pl.ds(spot, rg)], device)
        for device in gsend
    ]
    own = pl.multiple_of(y * ry, ry)
    for h in range(2):
        block = accw[h, pl.ds(own, ry), :]
        for w in ways:
            if w[0] == h:
                arrive([flying[w]])
                block = block + ring[slots[w + (hops[w],)]]
        ysum[h] = block
    wcopies = [
        send(
            ysum.at[lax.rem(q, 2), pl.ds(pl.multiple_of((q // 2) * rc, rc), rc)], zw.at[d], zldev[d]
        )
        for d, q in enumerate(zls)
    ]
    arrive(gcopies)
    quarter = pl.multiple_of(c * 64, 64)
    gcopies = [
        send(gfin.at[:, pl.ds(quarter, 64)], gfin.at[:, pl.ds(quarter, 64)], device)
        for device in xdev
    ]
    arrive(wcopies)
    piece = ysum[lax.rem(zl, 2), pl.ds(pl.multiple_of((zl // 2) * rc, rc), rc), :]
    for d in range(ZL - 1):
        piece = piece + zw[d]
    hw[zh] = piece
    wcopies = [send(hw.at[zh], hw.at[zh], device) for device in zhdev]
    arrive(gcopies)

    eye = jnp.where(
        lax.broadcasted_iota(jnp.int32, (HALF, HALF), 0)
        == lax.broadcasted_iota(jnp.int32, (HALF, HALF), 1),
        1.0,
        0.0,
    ).astype(F32)
    half_groups = HALF // 8
    place = [0]
    kept = []

    def advance(groups):
        while groups and place[0] < 2 * half_groups:
            if place[0] == 0:
                work[:, 0:HALF] = gfin[0, 0:HALF, :]
                work[:, HALF:] = eye
            if place[0] == half_groups:
                top = work[:, HALF:]
                low = exact(gfin[0, HALF:, :], top, NT)
                inv[0:HALF, 0:HALF] = top
                inv[0:HALF, HALF:] = jnp.zeros((HALF, HALF), F32)
                work[:, 0:HALF] = gfin[1, HALF:, :] - exact(low, low, NT)
                work[:, HALF:] = eye
                kept.append(exact(low, top, NN))
            first = place[0] % half_groups
            take = min(groups, half_groups - first)
            invert_factor(work, first, first + take)
            groups -= take
            place[0] += take

    advance(8)
    arrive(wcopies)
    piece = hw[0]
    for q in range(1, ZH):
        piece = piece + hw[q]
    spot = pl.multiple_of(core * HALF + y * ry + (zl // 2) * rc, rc)
    hz = lax.rem(zl, 2)
    full[hz, pl.ds(spot, rc), :] = piece
    wcopies = [
        send(full.at[hz, pl.ds(spot, rc)], full.at[hz, pl.ds(spot, rc)], device) for device in zldev
    ]
    advance(7)
    arrive(wcopies)

    def strip(h, sign, away):
        q = lax.rem(y - sign * away + Y, Y)
        return full.at[h, pl.ds(pl.multiple_of(mine + q * ry, ry), ry)]

    handed = []
    flying = {}

    def share(w, step):
        h, sign = w
        if step > 1:
            arrive([flying[w]])
        ref = strip(h, sign, step - 1)
        if step <= hops[w]:
            flying[w] = send(ref, ref, up if sign > 0 else down)
        if step > 1 or w in ((0, 1), (1, -1)):
            handed.append(send(ref, ref, twin))

    def share_step(step):
        for w in ways:
            if hops[w] + 1 >= step:
                share(w, step)

    share_step(1)
    advance(3)
    share_step(2)
    advance(5)
    share_step(3)
    advance(5)
    share_step(4)
    advance(4)
    share_step(5)
    last = work[:, HALF:]
    inv[HALF:, 0:HALF] = -exact(last, kept[0], NN)
    inv[HALF:, HALF:] = last

    whole = inv[...]
    arrive(handed)
    lanes_sum = jnp.zeros((R, HALF), F32)
    for h in range(2):
        value = triple(whole, full[h], NN)
        rt[h] = value
        for j in range(span // HALF):
            piece = value[:, HALF * j : HALF * (j + 1)]
            tiles[(span // HALF) * h + j] = piece
            lanes_sum = lanes_sum + piece * piece
    nz[c] = exact(jnp.ones((8, HALF), F32), lanes_sum, NT)
    copies = [send(nz.at[c], nz.at[c], device) for device in xdev]
    ortho = triple(proj, whole, NT)
    for h in range(2):
        lanes = slice(span * h, span * (h + 1))
        feedback = triple(ortho, rt[h], NN)
        new_momentum[:, lanes] = buf[0:rows, lanes] - feedback_share * feedback[0:rows]
    want = 5 * r + lax.broadcasted_iota(jnp.int32, (8, HALF), 0)
    have = lax.broadcasted_iota(jnp.int32, (8, HALF), 1)
    spot = (5 * r) // HALF
    picked = jnp.zeros((8, R), F32)
    for k in range(2):
        chosen = jnp.where(want == have + HALF * (spot + k), 1.0, 0.0).astype(F32)
        picked = picked + exact(chosen, tiles[jnp.minimum(spot + k, 2 * span // HALF - 1)], NT)
    arrive(copies)
    inverse = 1.0 / jnp.sqrt(((nz[0] + nz[1]) + (nz[2] + nz[3])) + epsilon)
    new_right[...] = (picked * inverse)[0:5].astype(BF16)
    scaled = ortho * inverse[0:1, :]
    scale = (M * N / R) ** 0.5
    for h in range(2):
        lanes = slice(span * h, span * (h + 1))
        update = triple(scaled, rt[h], NN)
        new_weight[:, lanes] = decay_keep * weight[:, lanes] - step_rate * scale * update[0:rows]
    for copy in sent:
        copy.wait_send()
    assert count[0] == ssem.shape[0]


def copies_of(Y, ZH):
    return 21 + 2 * (2 * Y - 1) + 2 * (ZH - 1) + 4 * (Y - 1) + 2 * Y


def on_device(dims, weight, grad, momentum, right_factor):
    Y, ZH = dims
    rows, width = weight.shape
    padded = -(-rows // 8) * 8
    span = width // 2
    ry = HALF // Y
    rc = ry // 2
    rg = 64 // Y
    total = copies_of(Y, ZH)
    vm = lambda *shape: pltpu.VMEM(shape, F32)
    scratch = [
        vm(padded, width), vm(2, padded, HALF), vm(2, padded, HALF), vm(4, padded, HALF),
        vm(2, padded, HALF), vm(2, HALF, span), vm(2, HALF, span), vm(2, HALF, span),
        vm(2 * (Y - 1), ry, span), vm(2, ry, span), vm(ZL - 1, rc, span), vm(ZH, rc, span),
        vm(2, R, span), vm(2, HALF, HALF), vm(2 * Y - 1, rg, HALF),
        vm(ZL, rg, HALF), vm(ZH, rg, HALF), vm(2, R, HALF), vm(HALF, 2 * HALF), vm(R, R),
        vm(2, R, span), vm(width // HALF, R, HALF), vm(4, 8, R),
        pltpu.SemaphoreType.DMA((total,)), pltpu.SemaphoreType.DMA((total,)),
    ]
    vmem = pl.BlockSpec(memory_space=pltpu.VMEM)
    return pl.pallas_call(
        functools.partial(kernel, dims),
        out_shape=(
            jax.ShapeDtypeStruct((rows, width), F32),
            jax.ShapeDtypeStruct((rows, width), F32),
            jax.ShapeDtypeStruct((5, R), BF16),
        ),
        in_specs=[vmem] * 4,
        out_specs=(vmem,) * 3,
        scratch_shapes=scratch,
        compiler_params=pltpu.CompilerParams(
            collective_id=0, has_side_effects=True, vmem_limit_bytes=60 * 1024 * 1024
        ),
        name="dion_step",
    )(weight, grad, momentum, right_factor)


def solution(mesh):
    placed = (P("row", "col"), P("row", "col"), P("row", "col"), P("col", None))
    return jax.shard_map(
        functools.partial(on_device, (8, 4)),
        mesh=mesh,
        in_specs=placed,
        out_specs=(P("row", "col"), P("row", "col"), P(("col", "row"), None)),
        check_vma=False,
    )
```

```python
import functools

import jax
import jax.numpy as jnp
from jax import lax
from jax.experimental import pallas as pl
from jax.experimental.pallas import tpu as pltpu
from jax.sharding import PartitionSpec as P

M = 25600
N = 5120
R = 256

feedback_share = 0.05
decay_keep = 0.999
step_rate = 0.5
epsilon = 1e-06

CORES = 2
ZL = 4
HALF = 128
PANEL = 32
F32 = jnp.float32
BF16 = jnp.bfloat16
NN = (((1,), (0,)), ((), ()))
NT = (((1,), (1,)), ((), ()))
TN = (((0,), (0,)), ((), ()))


def exact(a, b, dims):
    return lax.dot_general(a, b, dims, precision=lax.Precision.HIGHEST, preferred_element_type=F32)


def single(a, b, dims):
    return lax.dot_general(a, b, dims, preferred_element_type=F32)


def split(a):
    high = a.astype(BF16)
    return high, (a - high.astype(F32)).astype(BF16)


def triple(a, b, dims):
    ah, al = split(a)
    bh, bl = split(b)
    return single(ah, bh, dims) + (single(ah, bl, dims) + single(al, bh, dims))


def thirds(a):
    high = a.astype(BF16).astype(F32)
    rest = a - high
    middle = rest.astype(BF16).astype(F32)
    return high, middle, rest - middle


def invert_factor(work, first, last):
    lane = lax.broadcasted_iota(jnp.int32, (PANEL, HALF), 1)
    sub = lax.broadcasted_iota(jnp.int32, (PANEL, HALF), 0)

    def group(g, carry):
        base = pl.multiple_of(g * PANEL, PANEL)
        ra = work[pl.ds(base, PANEL), 0:HALF]
        rb = work[pl.ds(base, PANEL), HALF:]
        columns = [
            jnp.broadcast_to(
                jnp.sum(jnp.where(lane == base + i, ra, 0.0), axis=1, keepdims=True), (PANEL, HALF)
            )
            for i in range(PANEL)
        ]
        for i in range(PANEL):
            pivot = jnp.broadcast_to(columns[i][i : i + 1, :], (PANEL, HALF))
            s = lax.rsqrt(pivot)
            scaled = columns[i] * s
            below = jnp.where(sub > i, scaled, 0.0)
            for j in range(i + 1, PANEL):
                columns[j] = columns[j] - below * jnp.broadcast_to(scaled[j : j + 1, :], (PANEL, HALF))
            pa = jnp.broadcast_to(ra[i : i + 1, :], (PANEL, HALF)) * s
            pb = jnp.broadcast_to(rb[i : i + 1, :], (PANEL, HALF)) * s
            ra = jnp.where(sub == i, pa, ra - below * pa)
            rb = jnp.where(sub == i, pb, rb - below * pb)
        work[pl.ds(base, PANEL), 0:HALF] = ra
        work[pl.ds(base, PANEL), HALF:] = rb
        masked = jnp.where(lane >= base + PANEL, ra, 0.0)
        lh, lm, ll = thirds(masked)
        full = jnp.concatenate([ra, rb], axis=1)
        rh, rm, rl = thirds(full)
        left = jnp.concatenate([lh, lh, lm, lh, ll, lm], axis=0).astype(BF16)
        right = jnp.concatenate([rh, rm, rh, rl, rh, rm], axis=0).astype(BF16)
        work[...] = work[...] - single(left, right, TN)
        return carry

    lax.fori_loop(first, last, group, 0)


def kernel(
    dims, weight, grad, momentum, factor, new_weight, new_momentum, new_right,
    buf, part, both, rx, pr, wt, cw, accw, ring, ysum, zw, hw, full,
    gp, gy, gz, gh, gfin, work, inv, rt, tiles, nz, ssem, rsem,
):
    Y, ZH = dims
    rows = weight.shape[0]
    padded = buf.shape[0]
    span = weight.shape[1] // 2
    ry = HALF // Y
    rc = ry // 2
    rg = 64 // Y
    Z = ZH * ZL
    r = lax.axis_index("row")
    c = lax.axis_index("col")
    core = lax.rem(r, CORES)
    z = lax.rem(r // CORES, Z)
    y = r // (CORES * Z)
    zl = lax.rem(z, ZL)
    zh = z // ZL

    def at(y, z, core, c):
        return {"row": (y * Z + z) * CORES + core, "col": c}

    near = at(y, z, core, c + 1 - 2 * lax.rem(c, 2))
    far = at(y, z, core, 3 - c)
    twin = at(y, z, 1 - core, c)
    xdev = [at(y, z, core, lax.rem(c + d, 4)) for d in range(1, 4)]
    zls = [lax.rem(zl + d, ZL) for d in range(1, ZL)]
    zhs = [lax.rem(zh + d, ZH) for d in range(1, ZH)]
    group = [(d, k) for d in range(Y) for k in range(CORES) if d or k]
    gdev = []
    for d, k in group:
        gdev.append((lax.rem(y + d, Y), 1 - core if k else core))
    gsend = [at(q, z, k, c) for q, k in gdev]
    zldev = [at(y, zh * ZL + q, core, c) for q in zls]
    zhdev = [at(y, q * ZL + zl, core, c) for q in zhs]
    up, down = at(lax.rem(y + 1, Y), z, core, c), at(lax.rem(y + Y - 1, Y), z, core, c)
    hops = {(0, 1): Y // 2, (1, -1): Y // 2, (1, 1): Y // 2 - 1, (0, -1): Y // 2 - 1}
    ways = [w for w in hops if hops[w]]

    count = [0]
    sent = []

    def send(src, dst, device):
        k = count[0]
        count[0] += 1
        copy = pltpu.make_async_remote_copy(
            src_ref=src, dst_ref=dst, send_sem=ssem.at[k], recv_sem=rsem.at[k],
            device_id=device, device_id_type=pl.DeviceIdType.MESH,
        )
        copy.start()
        sent.append(copy)
        return copy

    def arrive(copies):
        for copy in copies:
            copy.wait_recv()

    barrier = pltpu.get_barrier_semaphore()
    peers = xdev + gsend + zldev + zhdev
    for device in peers:
        pl.semaphore_signal(barrier, inc=1, device_id=device, device_id_type=pl.DeviceIdType.MESH)

    buf[0:rows, :] = momentum[...] + grad[...]
    buf[rows:padded, :] = jnp.zeros((padded - rows, 2 * span), F32)
    value = buf[...]
    bh = value.astype(BF16)
    rest = value - bh.astype(F32)
    bm = rest.astype(BF16)
    bl = (rest - bm.astype(F32)).astype(BF16)
    fr = factor[...]
    partial_value = single(bh, fr, NN) + (single(bm, fr, NN) + single(bl, fr, NN))
    part[0] = partial_value[:, 0:HALF]
    part[1] = partial_value[:, HALF:]
    pl.semaphore_wait(barrier, len(peers))

    one = [send(part.at[0], rx.at[0], near), send(part.at[1], rx.at[1], far)]
    arrive(one)
    both[...] = part[...] + rx[0:2]
    two = [send(both.at[0], rx.at[2], far), send(both.at[1], rx.at[3], near)]
    arrive(two)
    pr[0] = both[0] + rx[2]
    pr[1] = both[1] + rx[3]
    proj = jnp.concatenate([pr[0], pr[1]], axis=1)

    gram = exact(pr[c // 2], proj, TN)
    gp[0] = gram[:, 0:HALF]
    gp[1] = gram[:, HALF:]
    inner = lax.rem(c, 2) * 64
    gcopies = [
        send(gp.at[k, pl.ds(pl.multiple_of(inner + q * rg, 8), rg)], gy.at[d], gsend[d])
        for d, (q, k) in enumerate(gdev)
    ]
    mine = pl.multiple_of(core * HALF, HALF)
    ph, pm = split(pr[1 - core])
    wcopies = []
    for h in range(2):
        b_h, b_l = split(buf[:, span * h : span * (h + 1)])
        wt[h] = single(ph, b_h, TN) + (single(ph, b_l, TN) + single(pm, b_h, TN))
        wcopies.append(send(wt.at[h], cw.at[h], twin))
    ph, pm = split(pr[core])
    for h in range(2):
        b_h, b_l = split(buf[:, span * h : span * (h + 1)])
        accw[h] = single(ph, b_h, TN) + (single(ph, b_l, TN) + single(pm, b_h, TN))
    arrive(gcopies)
    tile = gp[core, pl.ds(pl.multiple_of(inner + y * rg, 8), rg), :]
    for d in range(len(group)):
        tile = tile + gy[d]
    gz[zl] = tile
    gcopies = [send(gz.at[zl], gz.at[zl], device) for device in zldev]

    def chunk(h, sign, left):
        q = lax.rem(y + sign * left + Y, Y)
        return accw.at[h, pl.ds(pl.multiple_of(q * ry, ry), ry)]

    slots = {}
    for w in ways:
        for step in range(1, hops[w] + 1):
            slots[w + (step,)] = len(slots)
    flying = {}

    def pass_on(w, step):
        h, sign = w
        if step > 1:
            arrive([flying[w]])
            ref = chunk(h, sign, hops[w] + 1 - step)
            ref[...] = ref[...] + ring[slots[w + (step - 1,)]]
        flying[w] = send(
            chunk(h, sign, hops[w] + 1 - step), ring.at[slots[w + (step,)]], up if sign > 0 else down
        )

    for h in range(2):
        arrive([wcopies[h]])
        accw[h] = accw[h] + cw[h]
        for w in ways:
            if w[0] == h:
                pass_on(w, 1)

    def ring_step(step):
        for w in ways:
            if hops[w] >= step:
                pass_on(w, step)

    ring_step(2)
    arrive(gcopies)
    gh[zh] = (gz[0] + gz[1]) + (gz[2] + gz[3])
    gcopies = [send(gh.at[zh], gh.at[zh], device) for device in zhdev]
    ring_step(3)
    ring_step(4)
    own = pl.multiple_of(y * ry, ry)
    for h in range(2):
        block = accw[h, pl.ds(own, ry), :]
        for w in ways:
            if w[0] == h:
                arrive([flying[w]])
                block = block + ring[slots[w + (hops[w],)]]
        ysum[h] = block
    wcopies = [
        send(
            ysum.at[lax.rem(q, 2), pl.ds(pl.multiple_of((q // 2) * rc, rc), rc)], zw.at[d], zldev[d]
        )
        for d, q in enumerate(zls)
    ]
    arrive(gcopies)
    tile = gh[0]
    for q in range(1, ZH):
        tile = tile + gh[q]
    spot = pl.multiple_of(c * 64 + y * rg, 8)
    gfin[core, pl.ds(spot, rg), :] = tile
    gcopies = [
        send(gfin.at[core, pl.ds(spot, rg)], gfin.at[core, pl.ds(spot, rg)], device)
        for device in gsend
    ]
    arrive(wcopies)
    piece = ysum[lax.rem(zl, 2), pl.ds(pl.multiple_of((zl // 2) * rc, rc), rc), :]
    for d in range(ZL - 1):
        piece = piece + zw[d]
    hw[zh] = piece
    wcopies = [send(hw.at[zh], hw.at[zh], device) for device in zhdev]
    arrive(gcopies)
    quarter = pl.multiple_of(c * 64, 64)
    gcopies = [
        send(gfin.at[:, pl.ds(quarter, 64)], gfin.at[:, pl.ds(quarter, 64)], device)
        for device in xdev
    ]

    eye = jnp.where(
        lax.broadcasted_iota(jnp.int32, (HALF, HALF), 0)
        == lax.broadcasted_iota(jnp.int32, (HALF, HALF), 1),
        1.0,
        0.0,
    ).astype(F32)
    half_groups = HALF // PANEL
    place = [0]
    kept = []

    def advance(groups):
        while groups and place[0] < 2 * half_groups:
            if place[0] == 0:
                work[:, 0:HALF] = gfin[0, 0:HALF, :]
                work[:, HALF:] = eye
            if place[0] == half_groups:
                top = work[:, HALF:]
                low = exact(gfin[0, HALF:, :], top, NT)
                inv[0:HALF, 0:HALF] = top
                inv[0:HALF, HALF:] = jnp.zeros((HALF, HALF), F32)
                work[:, 0:HALF] = gfin[1, HALF:, :] - exact(low, low, NT)
                work[:, HALF:] = eye
                kept.append(exact(low, top, NN))
            first = place[0] % half_groups
            take = min(groups, half_groups - first)
            invert_factor(work, first, first + take)
            groups -= take
            place[0] += take

    arrive(wcopies)
    piece = hw[0]
    for q in range(1, ZH):
        piece = piece + hw[q]
    spot = pl.multiple_of(core * HALF + y * ry + (zl // 2) * rc, rc)
    hz = lax.rem(zl, 2)
    full[hz, pl.ds(spot, rc), :] = piece
    wcopies = [
        send(full.at[hz, pl.ds(spot, rc)], full.at[hz, pl.ds(spot, rc)], device) for device in zldev
    ]
    arrive(gcopies)
    advance(2)
    arrive(wcopies)

    def strip(h, sign, away):
        q = lax.rem(y - sign * away + Y, Y)
        return full.at[h, pl.ds(pl.multiple_of(mine + q * ry, ry), ry)]

    handed = []
    flying = {}

    def share(w, step):
        h, sign = w
        if step > 1:
            arrive([flying[w]])
        ref = strip(h, sign, step - 1)
        if step <= hops[w]:
            flying[w] = send(ref, ref, up if sign > 0 else down)
        if step > 1 or w in ((0, 1), (1, -1)):
            handed.append(send(ref, ref, twin))

    def share_step(step):
        for w in ways:
            if hops[w] + 1 >= step:
                share(w, step)

    share_step(1)
    advance(2)
    share_step(2)
    advance(1)
    share_step(3)
    advance(1)
    share_step(4)
    advance(2)
    share_step(5)
    last = work[:, HALF:]
    inv[HALF:, 0:HALF] = -exact(last, kept[0], NN)
    inv[HALF:, HALF:] = last

    whole = inv[...]
    arrive(handed)
    lanes_sum = jnp.zeros((R, HALF), F32)
    for h in range(2):
        value = triple(whole, full[h], NN)
        rt[h] = value
        for j in range(span // HALF):
            piece = value[:, HALF * j : HALF * (j + 1)]
            tiles[(span // HALF) * h + j] = piece
            lanes_sum = lanes_sum + piece * piece
    nz[c] = exact(jnp.ones((8, HALF), F32), lanes_sum, NT)
    copies = [send(nz.at[c], nz.at[c], device) for device in xdev]
    ortho = triple(proj, whole, NT)
    for h in range(2):
        lanes = slice(span * h, span * (h + 1))
        feedback = triple(ortho, rt[h], NN)
        new_momentum[:, lanes] = buf[0:rows, lanes] - feedback_share * feedback[0:rows]
    want = 5 * r + lax.broadcasted_iota(jnp.int32, (8, HALF), 0)
    have = lax.broadcasted_iota(jnp.int32, (8, HALF), 1)
    spot = (5 * r) // HALF
    picked = jnp.zeros((8, R), F32)
    for k in range(2):
        chosen = jnp.where(want == have + HALF * (spot + k), 1.0, 0.0).astype(F32)
        picked = picked + exact(chosen, tiles[jnp.minimum(spot + k, 2 * span // HALF - 1)], NT)
    arrive(copies)
    inverse = 1.0 / jnp.sqrt(((nz[0] + nz[1]) + (nz[2] + nz[3])) + epsilon)
    new_right[...] = (picked * inverse)[0:5].astype(BF16)
    scaled = ortho * inverse[0:1, :]
    scale = (M * N / R) ** 0.5
    for h in range(2):
        lanes = slice(span * h, span * (h + 1))
        update = triple(scaled, rt[h], NN)
        new_weight[:, lanes] = decay_keep * weight[:, lanes] - step_rate * scale * update[0:rows]
    for copy in sent:
        copy.wait_send()
    assert count[0] == ssem.shape[0]


def copies_of(Y, ZH):
    return 21 + 2 * (2 * Y - 1) + 2 * (ZH - 1) + 4 * (Y - 1) + 2 * Y


def on_device(dims, weight, grad, momentum, right_factor):
    Y, ZH = dims
    rows, width = weight.shape
    padded = -(-rows // 8) * 8
    span = width // 2
    ry = HALF // Y
    rc = ry // 2
    rg = 64 // Y
    total = copies_of(Y, ZH)
    vm = lambda *shape: pltpu.VMEM(shape, F32)
    scratch = [
        vm(padded, width), vm(2, padded, HALF), vm(2, padded, HALF), vm(4, padded, HALF),
        vm(2, padded, HALF), vm(2, HALF, span), vm(2, HALF, span), vm(2, HALF, span),
        vm(2 * (Y - 1), ry, span), vm(2, ry, span), vm(ZL - 1, rc, span), vm(ZH, rc, span),
        vm(2, R, span), vm(2, HALF, HALF), vm(2 * Y - 1, rg, HALF),
        vm(ZL, rg, HALF), vm(ZH, rg, HALF), vm(2, R, HALF), vm(HALF, 2 * HALF), vm(R, R),
        vm(2, R, span), vm(width // HALF, R, HALF), vm(4, 8, R),
        pltpu.SemaphoreType.DMA((total,)), pltpu.SemaphoreType.DMA((total,)),
    ]
    vmem = pl.BlockSpec(memory_space=pltpu.VMEM)
    return pl.pallas_call(
        functools.partial(kernel, dims),
        out_shape=(
            jax.ShapeDtypeStruct((rows, width), F32),
            jax.ShapeDtypeStruct((rows, width), F32),
            jax.ShapeDtypeStruct((5, R), BF16),
        ),
        in_specs=[vmem] * 4,
        out_specs=(vmem,) * 3,
        scratch_shapes=scratch,
        compiler_params=pltpu.CompilerParams(
            collective_id=0, has_side_effects=True, vmem_limit_bytes=60 * 1024 * 1024
        ),
        name="dion_step",
    )(weight, grad, momentum, right_factor)


def solution(mesh):
    placed = (P("row", "col"), P("row", "col"), P("row", "col"), P("col", None))
    return jax.shard_map(
        functools.partial(on_device, (8, 4)),
        mesh=mesh,
        in_specs=placed,
        out_specs=(P("row", "col"), P("row", "col"), P(("col", "row"), None)),
        check_vma=False,
    )
```

```python
import functools

import jax
import jax.numpy as jnp
from jax import lax
from jax.experimental import pallas as pl
from jax.experimental.pallas import tpu as pltpu
from jax.sharding import PartitionSpec as P

M = 25600
N = 5120
R = 256

feedback_share = 0.05
decay_keep = 0.999
step_rate = 0.5
epsilon = 1e-06

CORES = 2
ZL = 4
HALF = 128
PANEL = 32
F32 = jnp.float32
BF16 = jnp.bfloat16
NN = (((1,), (0,)), ((), ()))
NT = (((1,), (1,)), ((), ()))
TN = (((0,), (0,)), ((), ()))


def exact(a, b, dims):
    return lax.dot_general(a, b, dims, precision=lax.Precision.HIGHEST, preferred_element_type=F32)


def single(a, b, dims):
    return lax.dot_general(a, b, dims, preferred_element_type=F32)


def split(a):
    high = a.astype(BF16)
    return high, (a - high.astype(F32)).astype(BF16)


def triple(a, b, dims):
    ah, al = split(a)
    bh, bl = split(b)
    return single(ah, bh, dims) + (single(ah, bl, dims) + single(al, bh, dims))


def thirds(a):
    high = a.astype(BF16).astype(F32)
    rest = a - high
    middle = rest.astype(BF16).astype(F32)
    return high, middle, rest - middle


def invert_factor(work, first, last):
    lane = lax.broadcasted_iota(jnp.int32, (PANEL, HALF), 1)
    sub = lax.broadcasted_iota(jnp.int32, (PANEL, HALF), 0)

    def group(g, carry):
        base = pl.multiple_of(g * PANEL, PANEL)
        ra = work[pl.ds(base, PANEL), 0:HALF]
        rb = work[pl.ds(base, PANEL), HALF:]
        columns = [
            jnp.broadcast_to(
                jnp.sum(jnp.where(lane == base + i, ra, 0.0), axis=1, keepdims=True), (PANEL, HALF)
            )
            for i in range(PANEL)
        ]
        for i in range(PANEL):
            pivot = jnp.broadcast_to(columns[i][i : i + 1, :], (PANEL, HALF))
            s = lax.rsqrt(pivot)
            scaled = columns[i] * s
            below = jnp.where(sub > i, scaled, 0.0)
            for j in range(i + 1, PANEL):
                columns[j] = columns[j] - below * jnp.broadcast_to(scaled[j : j + 1, :], (PANEL, HALF))
            pa = jnp.broadcast_to(ra[i : i + 1, :], (PANEL, HALF)) * s
            pb = jnp.broadcast_to(rb[i : i + 1, :], (PANEL, HALF)) * s
            ra = jnp.where(sub == i, pa, ra - below * pa)
            rb = jnp.where(sub == i, pb, rb - below * pb)
        work[pl.ds(base, PANEL), 0:HALF] = ra
        work[pl.ds(base, PANEL), HALF:] = rb
        masked = jnp.where(lane >= base + PANEL, ra, 0.0)
        lh, lm, ll = thirds(masked)
        full = jnp.concatenate([ra, rb], axis=1)
        rh, rm, rl = thirds(full)
        left = jnp.concatenate([lh, lh, lm, lh, ll, lm], axis=0).astype(BF16)
        right = jnp.concatenate([rh, rm, rh, rl, rh, rm], axis=0).astype(BF16)
        work[...] = work[...] - single(left, right, TN)
        return carry

    lax.fori_loop(first, last, group, 0)


def kernel(
    dims, weight, grad, momentum, factor, new_weight, new_momentum, new_right,
    buf, part, both, rx, pr, wt, cw, accw, ring, ysum, zw, hw, full,
    gp, gy, gz, gh, gfin, work, inv, rt, tiles, nz, ssem, rsem,
):
    Y, ZH = dims
    rows = weight.shape[0]
    padded = buf.shape[0]
    span = weight.shape[1] // 2
    ry = HALF // Y
    rc = ry // 2
    rg = 64 // Y
    Z = ZH * ZL
    r = lax.axis_index("row")
    c = lax.axis_index("col")
    core = lax.rem(r, CORES)
    z = lax.rem(r // CORES, Z)
    y = r // (CORES * Z)
    zl = lax.rem(z, ZL)
    zh = z // ZL

    def at(y, z, core, c):
        return {"row": (y * Z + z) * CORES + core, "col": c}

    near = at(y, z, core, c + 1 - 2 * lax.rem(c, 2))
    far = at(y, z, core, 3 - c)
    twin = at(y, z, 1 - core, c)
    xdev = [at(y, z, core, lax.rem(c + d, 4)) for d in range(1, 4)]
    zls = [lax.rem(zl + d, ZL) for d in range(1, ZL)]
    zhs = [lax.rem(zh + d, ZH) for d in range(1, ZH)]
    group = [(d, k) for d in range(Y) for k in range(CORES) if d or k]
    gdev = []
    for d, k in group:
        gdev.append((lax.rem(y + d, Y), 1 - core if k else core))
    gsend = [at(q, z, k, c) for q, k in gdev]
    zldev = [at(y, zh * ZL + q, core, c) for q in zls]
    zhdev = [at(y, q * ZL + zl, core, c) for q in zhs]
    up, down = at(lax.rem(y + 1, Y), z, core, c), at(lax.rem(y + Y - 1, Y), z, core, c)
    hops = {(0, 1): Y // 2, (1, -1): Y // 2, (1, 1): Y // 2 - 1, (0, -1): Y // 2 - 1}
    ways = [w for w in hops if hops[w]]

    count = [0]
    sent = []

    def send(src, dst, device):
        k = count[0]
        count[0] += 1
        copy = pltpu.make_async_remote_copy(
            src_ref=src, dst_ref=dst, send_sem=ssem.at[k], recv_sem=rsem.at[k],
            device_id=device, device_id_type=pl.DeviceIdType.MESH,
        )
        copy.start()
        sent.append(copy)
        return copy

    def arrive(copies):
        for copy in copies:
            copy.wait_recv()

    barrier = pltpu.get_barrier_semaphore()
    peers = xdev + gsend + zldev + zhdev
    for device in peers:
        pl.semaphore_signal(barrier, inc=1, device_id=device, device_id_type=pl.DeviceIdType.MESH)

    buf[0:rows, :] = momentum[...] + grad[...]
    buf[rows:padded, :] = jnp.zeros((padded - rows, 2 * span), F32)
    value = buf[...]
    bh = value.astype(BF16)
    rest = value - bh.astype(F32)
    bm = rest.astype(BF16)
    bl = (rest - bm.astype(F32)).astype(BF16)
    fr = factor[...]
    partial_value = single(bh, fr, NN) + (single(bm, fr, NN) + single(bl, fr, NN))
    part[0] = partial_value[:, 0:HALF]
    part[1] = partial_value[:, HALF:]
    pl.semaphore_wait(barrier, len(peers))

    one = [send(part.at[0], rx.at[0], near), send(part.at[1], rx.at[1], far)]
    arrive(one)
    both[...] = part[...] + rx[0:2]
    two = [send(both.at[0], rx.at[2], far), send(both.at[1], rx.at[3], near)]
    arrive(two)
    pr[0] = both[0] + rx[2]
    pr[1] = both[1] + rx[3]
    proj = jnp.concatenate([pr[0], pr[1]], axis=1)

    gram = exact(pr[c // 2], proj, TN)
    gp[0] = gram[:, 0:HALF]
    gp[1] = gram[:, HALF:]
    inner = lax.rem(c, 2) * 64
    gcopies = [
        send(gp.at[k, pl.ds(pl.multiple_of(inner + q * rg, 8), rg)], gy.at[d], gsend[d])
        for d, (q, k) in enumerate(gdev)
    ]
    mine = pl.multiple_of(core * HALF, HALF)
    ph, pm = split(pr[1 - core])
    wcopies = []
    for h in range(2):
        b_h, b_l = split(buf[:, span * h : span * (h + 1)])
        wt[h] = single(ph, b_h, TN) + (single(ph, b_l, TN) + single(pm, b_h, TN))
        wcopies.append(send(wt.at[h], cw.at[h], twin))
    ph, pm = split(pr[core])
    for h in range(2):
        b_h, b_l = split(buf[:, span * h : span * (h + 1)])
        accw[h] = single(ph, b_h, TN) + (single(ph, b_l, TN) + single(pm, b_h, TN))
    arrive(gcopies)
    tile = gp[core, pl.ds(pl.multiple_of(inner + y * rg, 8), rg), :]
    for d in range(len(group)):
        tile = tile + gy[d]
    gz[zl] = tile
    gcopies = [send(gz.at[zl], gz.at[zl], device) for device in zldev]

    def chunk(h, sign, left):
        q = lax.rem(y + sign * left + Y, Y)
        return accw.at[h, pl.ds(pl.multiple_of(q * ry, ry), ry)]

    slots = {}
    for w in ways:
        for step in range(1, hops[w] + 1):
            slots[w + (step,)] = len(slots)
    flying = {}

    def pass_on(w, step):
        h, sign = w
        if step > 1:
            arrive([flying[w]])
            ref = chunk(h, sign, hops[w] + 1 - step)
            ref[...] = ref[...] + ring[slots[w + (step - 1,)]]
        flying[w] = send(
            chunk(h, sign, hops[w] + 1 - step), ring.at[slots[w + (step,)]], up if sign > 0 else down
        )

    for h in range(2):
        arrive([wcopies[h]])
        accw[h] = accw[h] + cw[h]
        for w in ways:
            if w[0] == h:
                pass_on(w, 1)

    def ring_step(step):
        for w in ways:
            if hops[w] >= step:
                pass_on(w, step)

    ring_step(2)
    arrive(gcopies)
    gh[zh] = (gz[0] + gz[1]) + (gz[2] + gz[3])
    gcopies = [send(gh.at[zh], gh.at[zh], device) for device in zhdev]
    ring_step(3)
    ring_step(4)
    own = pl.multiple_of(y * ry, ry)
    for h in range(2):
        block = accw[h, pl.ds(own, ry), :]
        for w in ways:
            if w[0] == h:
                arrive([flying[w]])
                block = block + ring[slots[w + (hops[w],)]]
        ysum[h] = block
    wcopies = [
        send(
            ysum.at[lax.rem(q, 2), pl.ds(pl.multiple_of((q // 2) * rc, rc), rc)], zw.at[d], zldev[d]
        )
        for d, q in enumerate(zls)
    ]
    arrive(gcopies)
    tile = gh[0]
    for q in range(1, ZH):
        tile = tile + gh[q]
    spot = pl.multiple_of(c * 64 + y * rg, 8)
    gfin[core, pl.ds(spot, rg), :] = tile
    gcopies = [
        send(gfin.at[core, pl.ds(spot, rg)], gfin.at[core, pl.ds(spot, rg)], device)
        for device in gsend
    ]
    arrive(wcopies)
    piece = ysum[lax.rem(zl, 2), pl.ds(pl.multiple_of((zl // 2) * rc, rc), rc), :]
    for d in range(ZL - 1):
        piece = piece + zw[d]
    hw[zh] = piece
    wcopies = [send(hw.at[zh], hw.at[zh], device) for device in zhdev]
    arrive(gcopies)
    quarter = pl.multiple_of(c * 64, 64)
    gcopies = [
        send(gfin.at[:, pl.ds(quarter, 64)], gfin.at[:, pl.ds(quarter, 64)], device)
        for device in xdev
    ]

    eye = jnp.where(
        lax.broadcasted_iota(jnp.int32, (HALF, HALF), 0)
        == lax.broadcasted_iota(jnp.int32, (HALF, HALF), 1),
        1.0,
        0.0,
    ).astype(F32)
    half_groups = HALF // PANEL
    place = [0]
    kept = []

    def advance(groups):
        while groups and place[0] < 2 * half_groups:
            if place[0] == 0:
                work[:, 0:HALF] = gfin[0, 0:HALF, :]
                work[:, HALF:] = eye
            if place[0] == half_groups:
                top = work[:, HALF:]
                low = exact(gfin[0, HALF:, :], top, NT)
                inv[0:HALF, 0:HALF] = top
                inv[0:HALF, HALF:] = jnp.zeros((HALF, HALF), F32)
                work[:, 0:HALF] = gfin[1, HALF:, :] - exact(low, low, NT)
                work[:, HALF:] = eye
                kept.append(exact(low, top, NN))
            first = place[0] % half_groups
            take = min(groups, half_groups - first)
            invert_factor(work, first, first + take)
            groups -= take
            place[0] += take

    arrive(wcopies)
    piece = hw[0]
    for q in range(1, ZH):
        piece = piece + hw[q]
    spot = pl.multiple_of(core * HALF + y * ry + (zl // 2) * rc, rc)
    hz = lax.rem(zl, 2)
    full[hz, pl.ds(spot, rc), :] = piece
    wcopies = [
        send(full.at[hz, pl.ds(spot, rc)], full.at[hz, pl.ds(spot, rc)], device) for device in zldev
    ]
    arrive(wcopies)

    def strip(h, sign, away):
        q = lax.rem(y - sign * away + Y, Y)
        return full.at[h, pl.ds(pl.multiple_of(mine + q * ry, ry), ry)]

    handed = []
    flying = {}

    def share(w, step):
        h, sign = w
        if step > 1:
            arrive([flying[w]])
        ref = strip(h, sign, step - 1)
        if step <= hops[w]:
            flying[w] = send(ref, ref, up if sign > 0 else down)
        if step > 1 or w in ((0, 1), (1, -1)):
            handed.append(send(ref, ref, twin))

    def share_step(step):
        for w in ways:
            if hops[w] + 1 >= step:
                share(w, step)

    share_step(1)
    arrive(gcopies)
    advance(3)
    share_step(2)
    advance(2)
    share_step(3)
    advance(2)
    share_step(4)
    advance(1)
    share_step(5)
    last = work[:, HALF:]
    inv[HALF:, 0:HALF] = -exact(last, kept[0], NN)
    inv[HALF:, HALF:] = last

    whole = inv[...]
    arrive(handed)
    lanes_sum = jnp.zeros((R, HALF), F32)
    for h in range(2):
        value = triple(whole, full[h], NN)
        rt[h] = value
        for j in range(span // HALF):
            piece = value[:, HALF * j : HALF * (j + 1)]
            tiles[(span // HALF) * h + j] = piece
            lanes_sum = lanes_sum + piece * piece
    nz[c] = exact(jnp.ones((8, HALF), F32), lanes_sum, NT)
    copies = [send(nz.at[c], nz.at[c], device) for device in xdev]
    ortho = triple(proj, whole, NT)
    for h in range(2):
        lanes = slice(span * h, span * (h + 1))
        feedback = triple(ortho, rt[h], NN)
        new_momentum[:, lanes] = buf[0:rows, lanes] - feedback_share * feedback[0:rows]
    want = 5 * r + lax.broadcasted_iota(jnp.int32, (8, HALF), 0)
    have = lax.broadcasted_iota(jnp.int32, (8, HALF), 1)
    spot = (5 * r) // HALF
    picked = jnp.zeros((8, R), F32)
    for k in range(2):
        chosen = jnp.where(want == have + HALF * (spot + k), 1.0, 0.0).astype(F32)
        picked = picked + exact(chosen, tiles[jnp.minimum(spot + k, 2 * span // HALF - 1)], NT)
    arrive(copies)
    inverse = 1.0 / jnp.sqrt(((nz[0] + nz[1]) + (nz[2] + nz[3])) + epsilon)
    new_right[...] = (picked * inverse)[0:5].astype(BF16)
    scaled = ortho * inverse[0:1, :]
    scale = (M * N / R) ** 0.5
    for h in range(2):
        lanes = slice(span * h, span * (h + 1))
        update = triple(scaled, rt[h], NN)
        new_weight[:, lanes] = decay_keep * weight[:, lanes] - step_rate * scale * update[0:rows]
    for copy in sent:
        copy.wait_send()
    assert count[0] == ssem.shape[0]


def copies_of(Y, ZH):
    return 21 + 2 * (2 * Y - 1) + 2 * (ZH - 1) + 4 * (Y - 1) + 2 * Y


def on_device(dims, weight, grad, momentum, right_factor):
    Y, ZH = dims
    rows, width = weight.shape
    padded = -(-rows // 8) * 8
    span = width // 2
    ry = HALF // Y
    rc = ry // 2
    rg = 64 // Y
    total = copies_of(Y, ZH)
    vm = lambda *shape: pltpu.VMEM(shape, F32)
    scratch = [
        vm(padded, width), vm(2, padded, HALF), vm(2, padded, HALF), vm(4, padded, HALF),
        vm(2, padded, HALF), vm(2, HALF, span), vm(2, HALF, span), vm(2, HALF, span),
        vm(2 * (Y - 1), ry, span), vm(2, ry, span), vm(ZL - 1, rc, span), vm(ZH, rc, span),
        vm(2, R, span), vm(2, HALF, HALF), vm(2 * Y - 1, rg, HALF),
        vm(ZL, rg, HALF), vm(ZH, rg, HALF), vm(2, R, HALF), vm(HALF, 2 * HALF), vm(R, R),
        vm(2, R, span), vm(width // HALF, R, HALF), vm(4, 8, R),
        pltpu.SemaphoreType.DMA((total,)), pltpu.SemaphoreType.DMA((total,)),
    ]
    vmem = pl.BlockSpec(memory_space=pltpu.VMEM)
    return pl.pallas_call(
        functools.partial(kernel, dims),
        out_shape=(
            jax.ShapeDtypeStruct((rows, width), F32),
            jax.ShapeDtypeStruct((rows, width), F32),
            jax.ShapeDtypeStruct((5, R), BF16),
        ),
        in_specs=[vmem] * 4,
        out_specs=(vmem,) * 3,
        scratch_shapes=scratch,
        compiler_params=pltpu.CompilerParams(
            collective_id=0, has_side_effects=True, vmem_limit_bytes=60 * 1024 * 1024
        ),
        name="dion_step",
    )(weight, grad, momentum, right_factor)


def solution(mesh):
    placed = (P("row", "col"), P("row", "col"), P("row", "col"), P("col", None))
    return jax.shard_map(
        functools.partial(on_device, (8, 4)),
        mesh=mesh,
        in_specs=placed,
        out_specs=(P("row", "col"), P("row", "col"), P(("col", "row"), None)),
        check_vma=False,
    )
```
